32 devices in a mesh: row: 4 (over y, x), col: 8 (over z, core).
Axes of the slice: x: 2, y: 2, z: 4, core: 2. Of those that a mesh axis runs over, the one named last changes fastest.
Arguments:
- activations: bfloat16 [512, 16384], P('col', 'row'), may hold values from -6 to 6
- grad_output: bfloat16 [512, 16384], P('col', 'row'), may hold values from -6 to 6
- gate_pre: bfloat16 [512, 8192], P('row', 'col'), may hold values from -8 to 8
- up_pre: bfloat16 [512, 8192], P('row', 'col'), may hold values from -6 to 6
- w_gate: bfloat16 [16384, 8192], P('row', 'col'), may hold values from -0.046875 to 0.046875
- w_up: bfloat16 [16384, 8192], P('row', 'col'), may hold values from -0.046875 to 0.046875
- w_down: bfloat16 [8192, 16384], P('col', 'row'), may hold values from -0.0625 to 0.0625
Outputs:
- grad_input: bfloat16 [512, 16384], P('col', 'row')
- grad_gate: bfloat16 [16384, 8192], P('row', 'col')
- grad_up: bfloat16 [16384, 8192], P('row', 'col')
- grad_down: bfloat16 [8192, 16384], P('col', 'row')
The draws below stay inside these ranges and needn't reach their ends.
All inputs are finite; a program needn't handle non-finite values.
Results may differ from the reference program's by a relative error of at most 0.005.
Values may be sent and summed in bfloat16 or wider, within the bound.
A program may use at most 128 MiB of HBM per device.

```python
import jax
import jax.numpy as jnp
from jax import lax

D = 16384
FF = 8192
TOKENS = 512


def block_scale(rng, dims, pieces, low, largest):
    gain = 1.0
    for axis_at, blocks in pieces:
        draws = jax.random.uniform(jax.random.fold_in(jax.random.fold_in(rng, 6), axis_at), (blocks,), jnp.float32, low / len(pieces), largest / len(pieces))
        gain = gain * jnp.repeat(jnp.exp(draws), dims[axis_at] // blocks).reshape((-1,) + (1,) * (len(dims) - 1 - axis_at))
    return gain


def normal_values(stream_key, shape, scale, reach, pieces=(), held_as=jnp.bfloat16):
    factor_of = block_scale(stream_key, shape, pieces, -0.22, 0.18) if pieces else 1.0
    values = jax.random.normal(stream_key, shape, jnp.float32) * scale * factor_of
    return jnp.minimum(jnp.maximum(values, -reach), reach).astype(held_as)


def setup_inputs(seed: int = 0) -> dict:
    splits = jax.random.split(jax.random.key(seed), 8)
    return {
        "activations": normal_values(splits[0], (TOKENS, D), 1.0, 6.0, ((0, 8), (1, 4))),
        "grad_output": normal_values(splits[1], (TOKENS, D), 1.0, 6.0, ((0, 8), (1, 4))),
        "gate_pre": normal_values(splits[2], (TOKENS, FF), 1.5, 8.0, ((0, 4), (1, 8))),
        "up_pre": normal_values(splits[3], (TOKENS, FF), 1.0, 6.0, ((0, 4), (1, 8))),
        "w_gate": normal_values(splits[4], (D, FF), D ** -0.5, 0.046875, ((0, 4), (1, 8))),
        "w_up": normal_values(splits[5], (D, FF), D ** -0.5, 0.046875, ((0, 4), (1, 8))),
        "w_down": normal_values(splits[6], (FF, D), FF ** -0.5, 0.0625, ((0, 8), (1, 4))),
    }


def reference(activations, grad_output, gate_pre, up_pre, w_gate, w_up, w_down):
    gate_val = gate_pre.astype(jnp.float32)
    up_val = up_pre.astype(jnp.float32)
    sigma = 1.0 / (1.0 + jnp.exp(-gate_val))
    hidden = (gate_val * sigma * up_val).astype(jnp.bfloat16)
    grad_hidden = lax.dot_general(grad_output, w_down, (((1,), (1,)), ((), ())), preferred_element_type=jnp.float32)
    grad_gate_pre = (grad_hidden * up_val * sigma * (1.0 + gate_val * (1.0 - sigma))).astype(jnp.bfloat16)
    grad_up_pre = (grad_hidden * gate_val * sigma).astype(jnp.bfloat16)
    contract_rows = (((0,), (0,)), ((), ()))
    grad_down = lax.dot_general(hidden, grad_output, contract_rows, preferred_element_type=jnp.float32).astype(jnp.bfloat16)
    grad_gate = lax.dot_general(activations, grad_gate_pre, contract_rows, preferred_element_type=jnp.float32).astype(jnp.bfloat16)
    grad_up = lax.dot_general(activations, grad_up_pre, contract_rows, preferred_element_type=jnp.float32).astype(jnp.bfloat16)
    contract_cols = (((1,), (1,)), ((), ()))
    grad_input = lax.dot_general(grad_gate_pre, w_gate, contract_cols, preferred_element_type=jnp.float32)
    grad_input = grad_input + lax.dot_general(grad_up_pre, w_up, contract_cols, preferred_element_type=jnp.float32)
    return grad_input.astype(jnp.bfloat16), grad_gate, grad_up, grad_down
```

```python
import functools

import jax
import jax.numpy as jnp
from jax import lax
from jax.experimental import pallas as pl
from jax.experimental.pallas import tpu as pltpu
from jax.sharding import PartitionSpec as P

MESH = pl.DeviceIdType.MESH
CONTRACT_COLS = (((1,), (1,)), ((), ()))
CONTRACT_ROWS = (((0,), (0,)), ((), ()))
F32 = jnp.float32
BF16 = jnp.bfloat16
PIECES = 2
COLUMN_TILES = 4


def tile_of(size, want):
    tile = min(size, want)
    while size % tile:
        tile //= 2
    return tile


def exchange_kernel(
    row_size, col_size,
    act_hbm, go_hbm, gate_hbm, up_hbm, wg_hbm, wu_hbm, wd_hbm,
    gi_out, go_hbm_out, act_hbm_out, hid_hbm, ggp_hbm, gup_hbm,
    go_all, act_all, hid_all, ggp_all, gup_all,
    wd, wg, wu, gate_all, up_all, part32, part16, rs_in, gh_all, gi, pair_in, z_in, z_out,
    ld, st, go_r, go_s, pg_r, pg_s, ac_r, ac_s, pa_r, pa_s, gu_r, gu_s,
    rs_r, rs_s, ag_r, ag_s, pr_r, pr_s, z_r, z_s,
):
    R, Z = row_size, col_size // 2
    shard, width = go_hbm.shape
    rows, feats = gate_hbm.shape
    chunk = 2 * shard
    own_rows = chunk // R
    ntiles = gi.shape[0]
    wt = width // ntiles
    piece = shard // PIECES

    r = lax.axis_index("row")
    c = lax.axis_index("col")
    z, k = c // 2, c % 2
    partner = (r, c + 1 - 2 * k)
    above = (r, c + 2)
    below = (r, c - 2)
    has_up = z < Z - 1
    has_dn = z > 0

    side_len = round(R ** 0.5)
    if side_len * side_len != R:
        side_len = 1
    lines = R // side_len
    row_a, row_b = r // lines, r % lines

    def peer(d):
        return (r + d) % R

    def remote(src, dst, ssem, rsem, dev):
        return pltpu.make_async_remote_copy(
            src_ref=src, dst_ref=dst, send_sem=ssem, recv_sem=rsem, device_id=dev, device_id_type=MESH
        )

    def ds(start, size, align=None):
        return pl.ds(pl.multiple_of(start, align or size), size)

    loads = [
        pltpu.make_async_copy(go_hbm, go_all.at[c], ld.at[0]),
        pltpu.make_async_copy(gate_hbm, gate_all.at[ds(r * rows, rows), :], ld.at[1]),
        pltpu.make_async_copy(up_hbm, up_all.at[ds(r * rows, rows), :], ld.at[2]),
        pltpu.make_async_copy(wd_hbm, wd, ld.at[3]),
        pltpu.make_async_copy(act_hbm, act_all.at[c], ld.at[4]),
        pltpu.make_async_copy(wg_hbm, wg, ld.at[5]),
        pltpu.make_async_copy(wu_hbm, wu, ld.at[6]),
    ]
    for load in loads:
        load.start()

    stores = [
        pltpu.make_async_copy(src, dst, st.at[i])
        for i, (src, dst) in enumerate((
            (go_all, go_hbm_out), (hid_all, hid_hbm), (ggp_all, ggp_hbm), (gup_all, gup_hbm), (act_all, act_hbm_out)
        ))
    ]

    barrier = pltpu.get_barrier_semaphore()

    def greet(dev):
        pl.semaphore_signal(barrier, inc=1, device_id=dev, device_id_type=MESH)

    greet(partner)
    for d in range(1, R):
        greet((peer(d), c))
    pl.when(has_up)(lambda: greet(above))
    pl.when(has_dn)(lambda: greet(below))
    pl.semaphore_wait(barrier, R + jnp.where(has_up, 1, 0) + jnp.where(has_dn, 1, 0))

    def go_z(direction, j, p):
        ref = go_all.at[2 * j + k, pl.ds(p * piece, piece)]
        return remote(ref, ref, go_s.at[direction, j, p], go_r.at[j, p], (above, below)[direction])

    def go_pair(j, side):
        ref = go_all.at[2 * j + side]
        return remote(ref, ref, pg_s.at[j], pg_r.at[j], partner)

    def act_z(direction, j):
        ref = act_all.at[2 * j + k]
        return remote(ref, ref, ac_s.at[direction, j], ac_r.at[j], (above, below)[direction])

    def act_pair(j, side):
        ref = act_all.at[2 * j + side]
        return remote(ref, ref, pa_s.at[j], pa_r.at[j], partner)

    def row_all(ref, ssem, rsem, d, start, size):
        part = ref.at[ds(start, size), :]
        return remote(part, part, ssem, rsem, (peer(d), c))

    def rows_wait(ref, ssem, rsem, size):
        part = ref.at[pl.ds(0, size), :]
        return remote(part, part, ssem, rsem, (peer(1), c))

    def start_act(direction):
        act_z(direction, z).start()

    loads[0].wait()

    @pl.when(has_up)
    def _():
        for p in range(PIECES):
            go_z(0, z, p).start()

    @pl.when(has_dn)
    def _():
        for p in range(PIECES):
            go_z(1, z, p).start()

    go_pair(z, k).start()
    loads[1].wait()
    loads[2].wait()
    half = rows // 2

    def saved(ref, sems, along, owner, part, d):
        block = ref.at[ds(owner * rows + part * half, half), :]
        if along == 0:
            dev = row_a * lines + (row_b + d) % lines
        else:
            dev = (row_a + d) % side_len * lines + row_b
        return remote(block, block, sems[0], sems[1], (dev, c))

    arrays = (gate_all, up_all)
    for i, ref in enumerate(arrays):
        for d in range(1, lines):
            saved(ref, (gu_s.at[i, 0], gu_r.at[i, 0]), 0, r, 0, d).start()
        for d in range(1, side_len):
            saved(ref, (gu_s.at[i, 1], gu_r.at[i, 1]), 1, r, 1, d).start()
    for i, ref in enumerate(arrays):
        for d in range(1, side_len):
            saved(ref, (gu_s.at[i, 2], gu_r.at[i, 2]), 1, r, 0, d).start()
        for d in range(1, lines):
            saved(ref, (gu_s.at[i, 3], gu_r.at[i, 3]), 0, r, 1, d).start()

    def saved_wait(i, stage, count):
        part = arrays[i].at[pl.ds(0, count * half), :]
        return remote(part, part, gu_s.at[i, stage], gu_r.at[i, stage], partner)

    def forward_saved():
        for i, ref in enumerate(arrays):
            if lines > 1:
                saved_wait(i, 0, lines - 1).wait_recv()
            for e in range(1, lines):
                owner = row_a * lines + (row_b + e) % lines
                for d in range(1, side_len):
                    saved(ref, (gu_s.at[i, 4], gu_r.at[i, 4]), 1, owner, 0, d).start()
            if side_len > 1:
                saved_wait(i, 1, side_len - 1).wait_recv()
            for e in range(1, side_len):
                owner = (row_a + e) % side_len * lines + row_b
                for d in range(1, lines):
                    saved(ref, (gu_s.at[i, 5], gu_r.at[i, 5]), 0, owner, 1, d).start()

    counts = (
        lines - 1, side_len - 1, side_len - 1, lines - 1,
        (lines - 1) * (side_len - 1), (lines - 1) * (side_len - 1),
    )
    loads[4].wait()
    act_pair(z, k).start()
    pl.when(has_up & (z == 0))(lambda: start_act(0))
    pl.when(has_dn & (z == Z - 1))(lambda: start_act(1))

    def forward(s):
        for p in range(PIECES):
            @pl.when(z - s >= 0)
            def _():
                j = z - s
                go_z(0, j, p).wait_recv()
                pl.when(has_up)(lambda: go_z(0, j, p).start())
                if p == PIECES - 1:
                    go_pair(j, k).start()
                    pl.when(has_up & (s == z))(lambda: start_act(0))

            @pl.when(z + s < Z)
            def _():
                j = z + s
                go_z(1, j, p).wait_recv()
                pl.when(has_dn)(lambda: go_z(1, j, p).start())
                if p == PIECES - 1:
                    go_pair(j, k).start()
                    pl.when(has_dn & (s == Z - 1 - z))(lambda: start_act(1))

    def act_forward(s):
        @pl.when(z - s >= 0)
        def _():
            j = z - s
            act_z(0, j).wait_recv()
            pl.when(has_up)(lambda: act_z(0, j).start())
            act_pair(j, k).start()

        @pl.when(z + s < Z)
        def _():
            j = z + s
            act_z(1, j).wait_recv()
            pl.when(has_dn)(lambda: act_z(1, j).start())
            act_pair(j, k).start()

    ftile = tile_of(feats, 256)

    def partial_hidden(j):
        go_pair(j, 1 - k).wait_recv()
        lhs = go_all[pl.ds(2 * j, 2)].reshape(chunk, width)

        @pl.loop(0, feats // ftile)
        def _(f):
            cols = ds(f * ftile, ftile)
            res = lax.dot_general(lhs, wd[cols, :], CONTRACT_COLS, preferred_element_type=F32)
            part32[ds(j * chunk, chunk), cols] = res
            part16[ds(j * chunk, chunk), cols] = res.astype(BF16)

        for d in range(1, R):
            src = part16.at[ds(j * chunk + peer(d) * own_rows, own_rows), :]
            dst = rs_in.at[ds((j * (R - 1) + d - 1) * own_rows, own_rows), :]
            remote(src, dst, rs_s.at[j], rs_r.at[j], (peer(d), c)).start()

    def finish_sum(j):
        rows_wait(rs_in, rs_s.at[j], rs_r.at[j], (R - 1) * own_rows).wait_recv()
        mine = ds(j * chunk + r * own_rows, own_rows)
        total = part32[mine, :]
        for d in range(1, R):
            total = total + rs_in[ds((j * (R - 1) + d - 1) * own_rows, own_rows), :].astype(F32)
        gh_all[mine, :] = total.astype(BF16)
        for d in range(1, R):
            row_all(gh_all, ag_s.at[j], ag_r.at[j], d, j * chunk + r * own_rows, own_rows).start()

    eblock = 16

    def finish_gather(j):
        rows_wait(gh_all, ag_s.at[j], ag_r.at[j], (R - 1) * own_rows).wait_recv()

        @pl.loop(0, chunk // eblock)
        def _(b):
            at = pl.ds(pl.multiple_of(j * chunk + b * eblock, eblock), eblock)
            gate = gate_all[at, :].astype(F32)
            up = up_all[at, :].astype(F32)
            grad = gh_all[at, :].astype(F32)
            sigma = 1.0 / (1.0 + jnp.exp(-gate))
            hid_all[at, :] = (gate * sigma * up).astype(BF16)
            ggp_all[at, :] = (grad * up * sigma * (1.0 + gate * (1.0 - sigma))).astype(BF16)
            gup_all[at, :] = (grad * gate * sigma).astype(BF16)

    def gathered_saved():
        for i in range(2):
            for stage in range(2, 6):
                if counts[stage]:
                    saved_wait(i, stage, counts[stage]).wait_recv()

    def at_distance(s, step):
        pl.when(z - s >= 0)(lambda: step(z - s))
        if s > 0:
            pl.when(z + s < Z)(lambda: step(z + s))

    for s in range(Z):
        if s > 0:
            forward(s)
        if s == 1:
            forward_saved()
        if s == 0:
            loads[3].wait()
        at_distance(s, partial_hidden)
        if s == Z - 1:
            act_forward(1)
        if s >= 1:
            at_distance(s - 1, finish_sum)
        if s == 2:
            gathered_saved()
        if s >= 2:
            at_distance(s - 2, finish_gather)
    if Z == 1:
        forward_saved()
    if Z <= 2:
        gathered_saved()
    at_distance(Z - 1, finish_sum)
    stores[0].start()
    if Z > 1:
        at_distance(Z - 2, finish_gather)
    at_distance(Z - 1, finish_gather)
    for store in stores[1:4]:
        store.start()

    loads[5].wait()
    loads[6].wait()
    gtile = tile_of(wt, 256)

    def input_tile(n):
        @pl.loop(0, wt // gtile)
        def _(t):
            at = ds(n * wt + t * gtile, gtile)
            res = lax.dot_general(ggp_all[...], wg[at, :], CONTRACT_COLS, preferred_element_type=F32)
            res = res + lax.dot_general(gup_all[...], wu[at, :], CONTRACT_COLS, preferred_element_type=F32)
            for j in range(Z):
                for side in range(2):
                    low_row = (2 * j + side) * shard
                    gi[n, side, j, :, ds(t * gtile, gtile)] = res[low_row : low_row + shard]

        pair_sum(n).start()

    def pair_sum(n):
        return remote(gi.at[n, 1 - k], pair_in.at[n], pr_s.at[n], pr_r.at[n], partner)

    def z_copy(n, j, slot, dev):
        return remote(z_out.at[n, j], z_in.at[n, slot], z_s.at[n, j], z_r.at[n, slot], dev)

    def pass_on(n, j, has_more, slot, dev):
        total = gi[n, k, j] + pair_in[n, j]

        @pl.when(has_more)
        def _():
            z_copy(n, j, j, dev).wait_recv()
            z_out[n, j] = (total + z_in[n, j].astype(F32)).astype(BF16)

        @pl.when(jnp.logical_not(has_more))
        def _():
            z_out[n, j] = total.astype(BF16)

        z_copy(n, j, slot, dev).start()

    lower = 2 * z < Z

    def serve_up(n, side):
        for j in range(Z - 1, 0, -1):
            pl.when((z < j) & (lower == side))(functools.partial(pass_on, n, j, has_dn, j, above))

    def serve(n):
        pair_sum(n).wait_recv()
        serve_up(n, True)
        for j in range(Z - 1):
            slot = jnp.where(z - 1 == j, Z, j)
            pl.when(z > j)(functools.partial(pass_on, n, j, has_up, slot, below))
        serve_up(n, False)

    def finish(n):
        total = gi[n, k, z] + pair_in[n, z]
        cols = pl.ds(n * wt, wt)
        gi[n, k, z] = total

        @pl.when(has_dn)
        def _():
            z_copy(n, z, z, below).wait_recv()
            gi[n, k, z] += z_in[n, z].astype(F32)

        @pl.when(has_up)
        def _():
            z_copy(n, z, Z, above).wait_recv()
            gi[n, k, z] += z_in[n, Z].astype(F32)

        gi_out[:, cols] = gi[n, k, z].astype(BF16)

    for n in range(ntiles):
        input_tile(n)
        if n >= 1:
            serve(n - 1)
        if n + 2 < Z and n >= 0:
            act_forward(n + 2)
    serve(ntiles - 1)
    for s in range(ntiles + 2, Z):
        act_forward(s)
    for n in range(ntiles):
        finish(n)

    for j in range(Z):
        act_pair(j, 1 - k).wait_recv()
    stores[4].start()
    for store in stores:
        store.wait()
    for j in range(Z):
        go_pair(j, k).wait_send()
        act_pair(j, k).wait_send()
        rows_wait(part16, rs_s.at[j], rs_r.at[j], (R - 1) * own_rows).wait_send()
        rows_wait(gh_all, ag_s.at[j], ag_r.at[j], (R - 1) * own_rows).wait_send()

        @pl.when((z >= j) & has_up)
        def _():
            for p in range(PIECES):
                go_z(0, j, p).wait_send()
            act_z(0, j).wait_send()

        @pl.when((z <= j) & has_dn)
        def _():
            for p in range(PIECES):
                go_z(1, j, p).wait_send()
            act_z(1, j).wait_send()

        @pl.when(z != j)
        def _():
            for n in range(ntiles):
                z_copy(n, j, j, partner).wait_send()

    for i in range(2):
        for stage in range(6):
            if counts[stage]:
                saved_wait(i, stage, counts[stage]).wait_send()
    for n in range(ntiles):
        pair_sum(n).wait_send()


def exchange(row_size, col_size, act, go, gate, up, wg, wu, wd):
    R, Z = row_size, col_size // 2
    shard, width = go.shape
    rows, feats = gate.shape
    tokens = shard * col_size
    own_rows = 2 * shard // R
    nt = COLUMN_TILES
    wt = width // nt
    hbm = pl.BlockSpec(memory_space=pltpu.HBM)
    vmem = pl.BlockSpec(memory_space=pltpu.VMEM)
    dma = pltpu.SemaphoreType.DMA
    sds = jax.ShapeDtypeStruct
    return pl.pallas_call(
        functools.partial(exchange_kernel, row_size, col_size),
        out_shape=[
            sds((shard, width), BF16),
            sds((col_size, shard, width), BF16),
            sds((col_size, shard, width), BF16),
            sds((tokens, feats), BF16),
            sds((tokens, feats), BF16),
            sds((tokens, feats), BF16),
        ],
        in_specs=[hbm] * 7,
        out_specs=[vmem] + [hbm] * 5,
        scratch_shapes=[
            pltpu.VMEM((col_size, shard, width), BF16),
            pltpu.VMEM((col_size, shard, width), BF16),
            pltpu.VMEM((tokens, feats), BF16),
            pltpu.VMEM((tokens, feats), BF16),
            pltpu.VMEM((tokens, feats), BF16),
            pltpu.VMEM(wd.shape, BF16),
            pltpu.VMEM(wg.shape, BF16),
            pltpu.VMEM(wu.shape, BF16),
            pltpu.VMEM((tokens, feats), BF16),
            pltpu.VMEM((tokens, feats), BF16),
            pltpu.VMEM((tokens, feats), F32),
            pltpu.VMEM((tokens, feats), BF16),
            pltpu.VMEM((Z * (R - 1) * own_rows, feats), BF16),
            pltpu.VMEM((tokens, feats), BF16),
            pltpu.VMEM((nt, 2, Z, shard, wt), F32),
            pltpu.VMEM((nt, Z, shard, wt), F32),
            pltpu.VMEM((nt, Z + 1, shard, wt), BF16),
            pltpu.VMEM((nt, Z, shard, wt), BF16),
            dma((7,)), dma((5,)),
            dma((Z, PIECES)), dma((2, Z, PIECES)), dma((Z,)), dma((Z,)),
            dma((Z,)), dma((2, Z)), dma((Z,)), dma((Z,)),
            dma((2, 6)), dma((2, 6)),
            dma((Z,)), dma((Z,)), dma((Z,)), dma((Z,)),
            dma((nt,)), dma((nt,)), dma((nt, Z + 1)), dma((nt, Z)),
        ],
        compiler_params=pltpu.CompilerParams(
            collective_id=0, has_side_effects=True, vmem_limit_bytes=67043328
        ),
        name="exchange",
    )(act, go, gate, up, wg, wu, wd)


def grads_kernel(tiles, lhs1, rhs1, lhs2, lhs3, rhs2, out1, out2, out3):
    i = pl.program_id(0)
    tokens = lhs1.shape[0]

    def product(lhs, rhs):
        return lax.dot_general(lhs, rhs, CONTRACT_ROWS, preferred_element_type=F32).astype(BF16)

    out1[...] = product(lhs1[...], rhs1[...].reshape(tokens, rhs1.shape[2]))
    rhs = rhs2[...].reshape(tokens, rhs2.shape[2])
    out2[...] = product(rhs, lhs2[...])
    out3[...] = product(rhs, lhs3[...])


def weight_grads(hid, go, act, ggp, gup):
    tokens, feats = hid.shape
    cols, shard, width = go.shape
    steps = min(8, feats // 128, width // 128)
    ft, wt = feats // steps, width // steps
    sds = jax.ShapeDtypeStruct
    vmem = pl.BlockSpec(memory_space=pltpu.VMEM)
    return pl.pallas_call(
        functools.partial(grads_kernel, steps),
        grid=(steps,),
        out_shape=[sds((feats, width), BF16), sds((width, feats), BF16), sds((width, feats), BF16)],
        in_specs=[
            pl.BlockSpec((tokens, ft), lambda i: (0, i)),
            pl.BlockSpec((cols, shard, width), lambda i: (0, 0, 0)),
            pl.BlockSpec((tokens, feats), lambda i: (0, 0)),
            pl.BlockSpec((tokens, feats), lambda i: (0, 0)),
            pl.BlockSpec((cols, shard, wt), lambda i: (0, 0, i)),
        ],
        out_specs=[
            pl.BlockSpec((ft, width), lambda i: (i, 0)),
            pl.BlockSpec((wt, feats), lambda i: (i, 0)),
            pl.BlockSpec((wt, feats), lambda i: (i, 0)),
        ],
        name="weight_grads",
    )(hid, go, ggp, gup, act)


def local(row_size, col_size, activations, grad_output, gate_pre, up_pre, w_gate, w_up, w_down):
    grad_input, go_all, act_all, hid, ggp, gup = exchange(
        row_size, col_size, activations, grad_output, gate_pre, up_pre, w_gate, w_up, w_down
    )
    grad_down, grad_gate, grad_up = weight_grads(hid, go_all, act_all, ggp, gup)
    return grad_input, grad_gate, grad_up, grad_down


def solution(mesh):
    in_specs = (
        P("col", "row"), P("col", "row"), P("row", "col"), P("row", "col"),
        P("row", "col"), P("row", "col"), P("col", "row"),
    )
    out_specs = (P("col", "row"), P("row", "col"), P("row", "col"), P("col", "row"))
    body = functools.partial(local, mesh.shape["row"], mesh.shape["col"])
    return jax.shard_map(body, mesh=mesh, in_specs=in_specs, out_specs=out_specs, check_vma=False)
```

```python
import functools

import jax
import jax.numpy as jnp
from jax import lax
from jax.experimental import pallas as pl
from jax.experimental.pallas import tpu as pltpu
from jax.sharding import PartitionSpec as P

MESH = pl.DeviceIdType.MESH
CONTRACT_COLS = (((1,), (1,)), ((), ()))
CONTRACT_ROWS = (((0,), (0,)), ((), ()))
F32 = jnp.float32
BF16 = jnp.bfloat16
PIECES = 2
COLUMN_TILES = 4


def tile_of(size, want):
    tile = min(size, want)
    while size % tile:
        tile //= 2
    return tile


def exchange_kernel(
    row_size, col_size,
    act_hbm, go_hbm, gate_hbm, up_hbm, wg_hbm, wu_hbm, wd_hbm,
    gi_out, wd, wg, act_all, gup_all,
    go_all, hid_all, ggp_all,
    wu, gate_all, up_all, part32, own32, part16, rs_in, gh_all, gi, pair_in, z_in, z_out,
    ld, go_r, go_s, pg_r, pg_s, ac_r, ac_s, pa_r, pa_s, gu_r, gu_s,
    rs_r, rs_s, ag_r, ag_s, pr_r, pr_s, z_r, z_s,
):
    R, Z = row_size, col_size // 2
    shard, width = go_hbm.shape
    rows, feats = gate_hbm.shape
    chunk = 2 * shard
    own_rows = chunk // R
    tokens = chunk * Z
    ntiles = gi.shape[0]
    wt = width // ntiles
    piece = shard // PIECES

    r = lax.axis_index("row")
    c = lax.axis_index("col")
    z, k = c // 2, c % 2
    partner = (r, c + 1 - 2 * k)
    above = (r, c + 2)
    below = (r, c - 2)
    has_up = z < Z - 1
    has_dn = z > 0

    side_len = round(R ** 0.5)
    if side_len * side_len != R:
        side_len = 1
    lines = R // side_len
    row_a, row_b = r // lines, r % lines

    def peer(d):
        return (r + d) % R

    def remote(src, dst, ssem, rsem, dev):
        return pltpu.make_async_remote_copy(
            src_ref=src, dst_ref=dst, send_sem=ssem, recv_sem=rsem, device_id=dev, device_id_type=MESH
        )

    def ds(start, size, align=None):
        return pl.ds(pl.multiple_of(start, align or size), size)

    loads = [
        pltpu.make_async_copy(go_hbm, go_all.at[c], ld.at[0]),
        pltpu.make_async_copy(gate_hbm, gate_all.at[ds(r * rows, rows), :], ld.at[1]),
        pltpu.make_async_copy(up_hbm, up_all.at[ds(r * rows, rows), :], ld.at[2]),
        pltpu.make_async_copy(wd_hbm, wd, ld.at[3]),
        pltpu.make_async_copy(act_hbm, act_all.at[c], ld.at[4]),
        pltpu.make_async_copy(wg_hbm, wg, ld.at[5]),
        pltpu.make_async_copy(wu_hbm, wu, ld.at[6]),
    ]
    for load in loads:
        load.start()

    barrier = pltpu.get_barrier_semaphore()

    def greet(dev):
        pl.semaphore_signal(barrier, inc=1, device_id=dev, device_id_type=MESH)

    greet(partner)
    for d in range(1, R):
        greet((peer(d), c))
    pl.when(has_up)(lambda: greet(above))
    pl.when(has_dn)(lambda: greet(below))
    pl.semaphore_wait(barrier, R + jnp.where(has_up, 1, 0) + jnp.where(has_dn, 1, 0))

    def go_z(direction, j, p):
        ref = go_all.at[2 * j + k, pl.ds(p * piece, piece)]
        return remote(ref, ref, go_s.at[direction, j, p], go_r.at[j, p], (above, below)[direction])

    def go_pair(j, side):
        ref = go_all.at[2 * j + side]
        return remote(ref, ref, pg_s.at[j], pg_r.at[j], partner)

    def act_z(direction, j):
        ref = act_all.at[2 * j + k]
        return remote(ref, ref, ac_s.at[direction, j], ac_r.at[j], (above, below)[direction])

    def act_pair(j, side):
        ref = act_all.at[2 * j + side]
        return remote(ref, ref, pa_s.at[j], pa_r.at[j], partner)

    def row_all(ref, ssem, rsem, d, start, size):
        part = ref.at[ds(start, size), :]
        return remote(part, part, ssem, rsem, (peer(d), c))

    def rows_wait(ref, ssem, rsem, size):
        part = ref.at[pl.ds(0, size), :]
        return remote(part, part, ssem, rsem, (peer(1), c))

    def start_act(direction):
        act_z(direction, z).start()

    loads[0].wait()

    @pl.when(has_up)
    def _():
        for p in range(PIECES):
            go_z(0, z, p).start()

    @pl.when(has_dn)
    def _():
        for p in range(PIECES):
            go_z(1, z, p).start()

    go_pair(z, k).start()
    loads[1].wait()
    loads[2].wait()
    half = rows // 2

    def saved(ref, sems, along, owner, part, d):
        block = ref.at[ds(owner * rows + part * half, half), :]
        if along == 0:
            dev = row_a * lines + (row_b + d) % lines
        else:
            dev = (row_a + d) % side_len * lines + row_b
        return remote(block, block, sems[0], sems[1], (dev, c))

    arrays = (gate_all, up_all)
    for i, ref in enumerate(arrays):
        for d in range(1, lines):
            saved(ref, (gu_s.at[i, 0], gu_r.at[i, 0]), 0, r, 0, d).start()
        for d in range(1, side_len):
            saved(ref, (gu_s.at[i, 1], gu_r.at[i, 1]), 1, r, 1, d).start()
    for i, ref in enumerate(arrays):
        for d in range(1, side_len):
            saved(ref, (gu_s.at[i, 2], gu_r.at[i, 2]), 1, r, 0, d).start()
        for d in range(1, lines):
            saved(ref, (gu_s.at[i, 3], gu_r.at[i, 3]), 0, r, 1, d).start()

    def saved_wait(i, stage, count):
        part = arrays[i].at[pl.ds(0, count * half), :]
        return remote(part, part, gu_s.at[i, stage], gu_r.at[i, stage], partner)

    def forward_saved():
        for i, ref in enumerate(arrays):
            if lines > 1:
                saved_wait(i, 0, lines - 1).wait_recv()
            for e in range(1, lines):
                owner = row_a * lines + (row_b + e) % lines
                for d in range(1, side_len):
                    saved(ref, (gu_s.at[i, 4], gu_r.at[i, 4]), 1, owner, 0, d).start()
            if side_len > 1:
                saved_wait(i, 1, side_len - 1).wait_recv()
            for e in range(1, side_len):
                owner = (row_a + e) % side_len * lines + row_b
                for d in range(1, lines):
                    saved(ref, (gu_s.at[i, 5], gu_r.at[i, 5]), 0, owner, 1, d).start()

    counts = (
        lines - 1, side_len - 1, side_len - 1, lines - 1,
        (lines - 1) * (side_len - 1), (lines - 1) * (side_len - 1),
    )
    loads[4].wait()
    act_pair(z, k).start()
    pl.when(has_up & (z == 0))(lambda: start_act(0))
    pl.when(has_dn & (z == Z - 1))(lambda: start_act(1))

    def forward(s):
        for p in range(PIECES):
            @pl.when(z - s >= 0)
            def _():
                j = z - s
                go_z(0, j, p).wait_recv()
                pl.when(has_up)(lambda: go_z(0, j, p).start())
                if p == PIECES - 1:
                    go_pair(j, k).start()
                    pl.when(has_up & (s == z))(lambda: start_act(0))

            @pl.when(z + s < Z)
            def _():
                j = z + s
                go_z(1, j, p).wait_recv()
                pl.when(has_dn)(lambda: go_z(1, j, p).start())
                if p == PIECES - 1:
                    go_pair(j, k).start()
                    pl.when(has_dn & (s == Z - 1 - z))(lambda: start_act(1))

    def act_from(direction, j, relay):
        act_z(direction, j).wait_recv()
        if relay:
            act_z(direction, j).start()
        act_pair(j, k).start()

    to_edge = jnp.minimum(z, Z - 1 - z)
    lower = 2 * z < Z
    edge = to_edge == 0

    def act_relay(t):
        near = t - to_edge
        far = t - (Z - 1 - to_edge)
        near_ok = (near >= 1) & (near <= to_edge)
        far_ok = (far >= 1) & (far <= Z - 1 - to_edge) & jnp.logical_not(edge)
        pl.when(near_ok & lower)(lambda: act_from(0, z - near, True))
        pl.when(near_ok & jnp.logical_not(lower))(lambda: act_from(1, z + near, True))
        pl.when(far_ok & lower)(lambda: act_from(1, z + far, True))
        pl.when(far_ok & jnp.logical_not(lower))(lambda: act_from(0, z - far, True))

    def act_end(s):
        pl.when(edge & (z - s >= 0))(lambda: act_from(0, z - s, False))
        pl.when(edge & (z + s < Z))(lambda: act_from(1, z + s, False))

    ftile = tile_of(feats, 256)

    def partial_hidden(j):
        go_pair(j, 1 - k).wait_recv()
        lhs = go_all[pl.ds(2 * j, 2)].reshape(chunk, width)

        @pl.loop(0, feats // ftile)
        def _(f):
            cols = ds(f * ftile, ftile)
            res = lax.dot_general(lhs, wd[cols, :], CONTRACT_COLS, preferred_element_type=F32)
            part32[:, cols] = res
            part16[ds(j * chunk, chunk), cols] = res.astype(BF16)

        own32[ds(j * own_rows, own_rows), :] = part32[ds(r * own_rows, own_rows), :]
        for d in range(1, R):
            src = part16.at[ds(j * chunk + peer(d) * own_rows, own_rows), :]
            dst = rs_in.at[ds((j * (R - 1) + d - 1) * own_rows, own_rows), :]
            remote(src, dst, rs_s.at[j], rs_r.at[j], (peer(d), c)).start()

    def finish_sum(j):
        rows_wait(rs_in, rs_s.at[j], rs_r.at[j], (R - 1) * own_rows).wait_recv()
        mine = ds(j * chunk + r * own_rows, own_rows)
        total = own32[ds(j * own_rows, own_rows), :]
        for d in range(1, R):
            total = total + rs_in[ds((j * (R - 1) + d - 1) * own_rows, own_rows), :].astype(F32)
        gh_all[mine, :] = total.astype(BF16)
        for d in range(1, R):
            row_all(gh_all, ag_s.at[j], ag_r.at[j], d, j * chunk + r * own_rows, own_rows).start()

    eblock = 16

    def finish_gather(j):
        rows_wait(gh_all, ag_s.at[j], ag_r.at[j], (R - 1) * own_rows).wait_recv()

        @pl.loop(0, chunk // eblock)
        def _(b):
            at = pl.ds(pl.multiple_of(j * chunk + b * eblock, eblock), eblock)
            gate = gate_all[at, :].astype(F32)
            up = up_all[at, :].astype(F32)
            grad = gh_all[at, :].astype(F32)
            sigma = 1.0 / (1.0 + jnp.exp(-gate))
            hid_all[at, :] = (gate * sigma * up).astype(BF16)
            ggp_all[at, :] = (grad * up * sigma * (1.0 + gate * (1.0 - sigma))).astype(BF16)
            gup_all[at, :] = (grad * gate * sigma).astype(BF16)

    def gathered_saved():
        for i in range(2):
            for stage in range(2, 6):
                if counts[stage]:
                    saved_wait(i, stage, counts[stage]).wait_recv()

    def at_distance(s, step):
        pl.when(z - s >= 0)(lambda: step(z - s))
        if s > 0:
            pl.when(z + s < Z)(lambda: step(z + s))

    for s in range(Z):
        if s > 0:
            forward(s)
        if s == 0:
            loads[3].wait()
        at_distance(s, partial_hidden)
        if s == 1:
            forward_saved()
        if s >= 2:
            act_relay(s)
        if s > 0:
            pl.when(jnp.logical_not(edge))(lambda: at_distance(s - 1, finish_sum))
        if s == 2:
            gathered_saved()
            at_distance(0, finish_gather)
            pl.when(edge)(lambda: at_distance(1, finish_gather))
        if s > 2:
            pl.when(jnp.logical_not(edge))(lambda: at_distance(s - 2, finish_gather))
            pl.when(edge)(lambda: at_distance(s - 1, finish_gather))
        if s < Z - 1:
            pl.when(edge)(lambda: at_distance(s, finish_sum))
    if Z == 2:
        gathered_saved()
        at_distance(0, finish_gather)
    if Z > 2:
        pl.when(jnp.logical_not(edge))(lambda: at_distance(Z - 2, finish_gather))

    loads[5].wait()
    loads[6].wait()
    gtile = tile_of(wt, 256)

    first = jnp.where(lower, 0, 1)
    last = jnp.where(lower, Z - 1, 0)

    def input_tile(n, start, count):
        rows_at = ds(start * chunk, count * chunk, chunk)

        @pl.loop(0, wt // gtile)
        def _(t):
            at = ds(n * wt + t * gtile, gtile)
            res = lax.dot_general(ggp_all[rows_at, :], wg[at, :], CONTRACT_COLS, preferred_element_type=F32)
            res = res + lax.dot_general(gup_all[rows_at, :], wu[at, :], CONTRACT_COLS, preferred_element_type=F32)
            for j in range(count):
                for side in range(2):
                    low_row = (2 * j + side) * shard
                    gi[n, side, start + j, :, ds(t * gtile, gtile)] = res[low_row : low_row + shard]

    def pair_sum(n, late):
        at = pl.ds(last, 1) if late else pl.ds(first, Z - 1)
        return remote(gi.at[n, 1 - k, at], pair_in.at[n, at], pr_s.at[late, n], pr_r.at[late, n], partner)

    def early(n):
        input_tile(n, first, Z - 1)
        pair_sum(n, 0).start()

    def late(n):
        input_tile(n, last, 1)
        pair_sum(n, 1).start()

    def z_copy(n, j, slot, dev):
        return remote(z_out.at[n, j], z_in.at[n, slot], z_s.at[n, j], z_r.at[n, slot], dev)

    def pass_on(n, j, fed, slot, dev):
        total = gi[n, k, j] + pair_in[n, j]
        if fed:
            z_copy(n, j, j, dev).wait_recv()
            total = total + z_in[n, j].astype(F32)
        z_out[n, j] = total.astype(BF16)
        z_copy(n, j, slot, dev).start()

    def move_up(n, j, fed):
        pass_on(n, j, fed, j, above)

    def move_down(n, j, fed):
        pass_on(n, j, fed, jnp.where(z - 1 == j, Z, j), below)

    def edge_serve(n, is_late):
        pair_sum(n, is_late).wait_recv()
        for j in [Z - 1] if is_late else range(Z - 2, 0, -1):
            pl.when(lower)(functools.partial(move_up, n, j, False))
        for j in [0] if is_late else range(1, Z - 1):
            pl.when(jnp.logical_not(lower))(functools.partial(move_down, n, j, False))

    def mid_early(n):
        pair_sum(n, 0).wait_recv()

        def ups(side):
            for j in range(Z - 2, 1, -1):
                pl.when((z < j) & (lower == side))(functools.partial(move_up, n, j, True))

        ups(True)
        for j in range(1, Z - 2):
            pl.when(z > j)(functools.partial(move_down, n, j, True))
        ups(False)

    def mid_late(n, near):
        if near:
            pair_sum(n, 1).wait_recv()
        pl.when(lower == near)(functools.partial(move_up, n, Z - 1, True))
        pl.when(lower != near)(functools.partial(move_down, n, 0, True))

    def finish(n):
        total = gi[n, k, z] + pair_in[n, z]
        cols = pl.ds(n * wt, wt)
        gi[n, k, z] = total

        @pl.when(has_dn)
        def _():
            z_copy(n, z, z, below).wait_recv()
            gi[n, k, z] += z_in[n, z].astype(F32)

        @pl.when(has_up)
        def _():
            z_copy(n, z, Z, above).wait_recv()
            gi[n, k, z] += z_in[n, Z].astype(F32)

        gi_out[:, cols] = gi[n, k, z].astype(BF16)

    blocks = 4
    fb = feats // blocks
    wb = width // blocks
    nb = tile_of(width, 1024)

    def down_block(i):
        rows_at = pl.ds(i * fb, fb)

        @pl.loop(0, width // nb)
        def _(t):
            cols = ds(t * nb, nb)
            rhs = go_all[:, :, cols].reshape(tokens, nb)
            wd[rows_at, cols] = lax.dot_general(
                hid_all[:, rows_at], rhs, CONTRACT_ROWS, preferred_element_type=F32
            ).astype(BF16)

    def gate_block(i):
        gb = tile_of(wb, 256)

        @pl.loop(0, wb // gb)
        def _(t):
            cols = ds(i * wb + t * gb, gb)
            lhs = act_all[:, :, cols].reshape(tokens, gb)
            wg[cols, :] = lax.dot_general(
                lhs, ggp_all[...], CONTRACT_ROWS, preferred_element_type=F32
            ).astype(BF16)

    early(0)

    @pl.when(edge)
    def _():
        edge_serve(0, 0)
        at_distance(Z - 1, finish_sum)
        early(1)
        at_distance(Z - 1, finish_gather)
        late(0)
        for n in range(1, ntiles):
            edge_serve(n, 0)
            edge_serve(n - 1, 1)
            if n + 1 < ntiles:
                early(n + 1)
            late(n)
        edge_serve(ntiles - 1, 1)

    @pl.when(jnp.logical_not(edge))
    def _():
        at_distance(Z - 1, finish_sum)
        mid_early(0)
        act_relay(Z)
        early(1)
        at_distance(Z - 1, finish_gather)
        late(0)
        for n in range(1, ntiles):
            if n + 1 < ntiles:
                early(n + 1)
            mid_early(n)
            late(n)
            down_block(n - 1)
            mid_late(n - 1, True)
            if n > 1:
                mid_late(n - 2, False)
            act_relay(Z + n)
        for n in (ntiles - 1, ntiles):
            if n < ntiles:
                down_block(n)
                mid_late(n, True)
            mid_late(n - 1, False)
        for t in range(Z + ntiles, 2 * Z - 2):
            act_relay(t)

    for s in range(1, Z):
        act_end(s)
    for j in range(Z):
        act_pair(j, 1 - k).wait_recv()

    @pl.when(edge)
    def _():
        for i in range(blocks):
            down_block(i)

    for n in range(ntiles):
        finish(n)
        for i in range(n * blocks // ntiles, (n + 1) * blocks // ntiles):
            gate_block(i)

    for j in range(Z):
        go_pair(j, k).wait_send()
        act_pair(j, k).wait_send()
        rows_wait(part16, rs_s.at[j], rs_r.at[j], (R - 1) * own_rows).wait_send()
        rows_wait(gh_all, ag_s.at[j], ag_r.at[j], (R - 1) * own_rows).wait_send()

        @pl.when((z >= j) & has_up)
        def _():
            for p in range(PIECES):
                go_z(0, j, p).wait_send()
            act_z(0, j).wait_send()

        @pl.when((z <= j) & has_dn)
        def _():
            for p in range(PIECES):
                go_z(1, j, p).wait_send()
            act_z(1, j).wait_send()

        @pl.when(z != j)
        def _():
            for n in range(ntiles):
                z_copy(n, j, j, partner).wait_send()

    for i in range(2):
        for stage in range(6):
            if counts[stage]:
                saved_wait(i, stage, counts[stage]).wait_send()
    for n in range(ntiles):
        pair_sum(n, 0).wait_send()
        pair_sum(n, 1).wait_send()


def exchange(row_size, col_size, act, go, gate, up, wg, wu, wd):
    R, Z = row_size, col_size // 2
    shard, width = go.shape
    rows, feats = gate.shape
    tokens = shard * col_size
    own_rows = 2 * shard // R
    nt = COLUMN_TILES
    wt = width // nt
    hbm = pl.BlockSpec(memory_space=pltpu.HBM)
    vmem = pl.BlockSpec(memory_space=pltpu.VMEM)
    dma = pltpu.SemaphoreType.DMA
    sds = jax.ShapeDtypeStruct
    return pl.pallas_call(
        functools.partial(exchange_kernel, row_size, col_size),
        out_shape=[
            sds((shard, width), BF16),
            pltpu.VMEM(wd.shape, BF16),
            pltpu.VMEM(wg.shape, BF16),
            pltpu.VMEM((col_size, shard, width), BF16),
            pltpu.VMEM((tokens, feats), BF16),
        ],
        in_specs=[hbm] * 7,
        out_specs=[vmem] * 5,
        scratch_shapes=[
            pltpu.VMEM((col_size, shard, width), BF16),
            pltpu.VMEM((tokens, feats), BF16),
            pltpu.VMEM((tokens, feats), BF16),
            pltpu.VMEM(wu.shape, BF16),
            pltpu.VMEM((tokens, feats), BF16),
            pltpu.VMEM((tokens, feats), BF16),
            pltpu.VMEM((2 * shard, feats), F32),
            pltpu.VMEM((Z * own_rows, feats), F32),
            pltpu.VMEM((tokens, feats), BF16),
            pltpu.VMEM((Z * (R - 1) * own_rows, feats), BF16),
            pltpu.VMEM((tokens, feats), BF16),
            pltpu.VMEM((nt, 2, Z, shard, wt), F32),
            pltpu.VMEM((nt, Z, shard, wt), F32),
            pltpu.VMEM((nt, Z + 1, shard, wt), BF16),
            pltpu.VMEM((nt, Z, shard, wt), BF16),
            dma((7,)),
            dma((Z, PIECES)), dma((2, Z, PIECES)), dma((Z,)), dma((Z,)),
            dma((Z,)), dma((2, Z)), dma((Z,)), dma((Z,)),
            dma((2, 6)), dma((2, 6)),
            dma((Z,)), dma((Z,)), dma((Z,)), dma((Z,)),
            dma((2, nt)), dma((2, nt)), dma((nt, Z + 1)), dma((nt, Z)),
        ],
        compiler_params=pltpu.CompilerParams(
            collective_id=0, has_side_effects=True, vmem_limit_bytes=39 << 20
        ),
        name="exchange",
    )(*(pltpu.with_memory_space_constraint(x, pltpu.HBM) for x in (act, go, gate, up, wg, wu, wd)))


def last_kernel(steps, lhs, rhs, down, gate, out, down_out, gate_out, sems):
    i = pl.program_id(0)
    copies = [
        pltpu.make_async_copy(down, down_out, sems.at[0]),
        pltpu.make_async_copy(gate, gate_out, sems.at[1]),
    ]

    @pl.when(i == 0)
    def _():
        for copy in copies:
            copy.start()

    cols = pl.ds(pl.multiple_of(i * out.shape[0], out.shape[0]), out.shape[0])
    out[...] = lax.dot_general(
        lhs[:, :, cols].reshape(rhs.shape[0], out.shape[0]), rhs[...], CONTRACT_ROWS, preferred_element_type=F32
    ).astype(BF16)

    @pl.when(i == steps - 1)
    def _():
        for copy in copies:
            copy.wait()


def last_grad(act, gup, down, gate):
    cols, shard, width = act.shape
    tokens, feats = gup.shape
    tile = tile_of(width, 512)
    steps = width // tile
    sds = jax.ShapeDtypeStruct
    vmem = pl.BlockSpec(memory_space=pltpu.VMEM)
    hbm = pl.BlockSpec(memory_space=pltpu.HBM)
    return pl.pallas_call(
        functools.partial(last_kernel, steps),
        grid=(steps,),
        out_shape=[sds((width, feats), BF16), sds(down.shape, BF16), sds(gate.shape, BF16)],
        in_specs=[
            vmem,
            vmem,
            vmem,
            vmem,
        ],
        out_specs=[pl.BlockSpec((tile, feats), lambda i: (i, 0)), hbm, hbm],
        scratch_shapes=[pltpu.SemaphoreType.DMA((2,))],
        compiler_params=pltpu.CompilerParams(vmem_limit_bytes=16 << 20),
        name="last_grad",
    )(*(pltpu.with_memory_space_constraint(x, pltpu.VMEM) for x in (act, gup, down, gate)))


def local(row_size, col_size, activations, grad_output, gate_pre, up_pre, w_gate, w_up, w_down):
    grad_input, grad_down, grad_gate, act_all, gup = exchange(
        row_size, col_size, activations, grad_output, gate_pre, up_pre, w_gate, w_up, w_down
    )
    grad_up, grad_down, grad_gate = last_grad(act_all, gup, grad_down, grad_gate)
    return grad_input, grad_gate, grad_up, grad_down


def solution(mesh):
    in_specs = (
        P("col", "row"), P("col", "row"), P("row", "col"), P("row", "col"),
        P("row", "col"), P("row", "col"), P("col", "row"),
    )
    out_specs = (P("col", "row"), P("row", "col"), P("row", "col"), P("col", "row"))
    body = functools.partial(local, mesh.shape["row"], mesh.shape["col"])
    return jax.shard_map(body, mesh=mesh, in_specs=in_specs, out_specs=out_specs, check_vma=False)
```

```python
import functools

import jax
import jax.numpy as jnp
from jax import lax
from jax.experimental import pallas as pl
from jax.experimental.pallas import tpu as pltpu
from jax.sharding import PartitionSpec as P

MESH = pl.DeviceIdType.MESH
CONTRACT_COLS = (((1,), (1,)), ((), ()))
CONTRACT_ROWS = (((0,), (0,)), ((), ()))
F32 = jnp.float32
BF16 = jnp.bfloat16
PIECES = 2
COLUMN_TILES = 4


def tile_of(size, want):
    tile = min(size, want)
    while size % tile:
        tile //= 2
    return tile


def exchange_kernel(
    row_size, col_size,
    act_hbm, go_hbm, gate_hbm, up_hbm, wg_hbm, wu_hbm, wd_hbm,
    gi_out, wd, wg, act_all, gup_all,
    go_all, hid_all, ggp_all,
    wu, gate_all, up_all, part32, own32, part16, rs_in, gh_all, gi, pair_in, z_in, z_out,
    ld, go_r, go_s, pg_r, pg_s, ac_r, ac_s, pa_r, pa_s, gu_r, gu_s,
    rs_r, rs_s, ag_r, ag_s, pr_r, pr_s, z_r, z_s,
):
    R, Z = row_size, col_size // 2
    shard, width = go_hbm.shape
    rows, feats = gate_hbm.shape
    chunk = 2 * shard
    own_rows = chunk // R
    tokens = chunk * Z
    ntiles = gi.shape[0]
    wt = width // ntiles
    piece = shard // PIECES

    r = lax.axis_index("row")
    c = lax.axis_index("col")
    z, k = c // 2, c % 2
    partner = (r, c + 1 - 2 * k)
    above = (r, c + 2)
    below = (r, c - 2)
    has_up = z < Z - 1
    has_dn = z > 0

    side_len = round(R ** 0.5)
    if side_len * side_len != R:
        side_len = 1
    lines = R // side_len
    row_a, row_b = r // lines, r % lines

    def peer(d):
        return (r + d) % R

    def remote(src, dst, ssem, rsem, dev):
        return pltpu.make_async_remote_copy(
            src_ref=src, dst_ref=dst, send_sem=ssem, recv_sem=rsem, device_id=dev, device_id_type=MESH
        )

    def ds(start, size, align=None):
        return pl.ds(pl.multiple_of(start, align or size), size)

    loads = [
        pltpu.make_async_copy(go_hbm, go_all.at[c], ld.at[0]),
        pltpu.make_async_copy(gate_hbm, gate_all.at[ds(r * rows, rows), :], ld.at[1]),
        pltpu.make_async_copy(up_hbm, up_all.at[ds(r * rows, rows), :], ld.at[2]),
        pltpu.make_async_copy(wd_hbm, wd, ld.at[3]),
        pltpu.make_async_copy(act_hbm, act_all.at[c], ld.at[4]),
        pltpu.make_async_copy(wg_hbm, wg, ld.at[5]),
        pltpu.make_async_copy(wu_hbm, wu, ld.at[6]),
    ]
    for load in loads:
        load.start()

    barrier = pltpu.get_barrier_semaphore()

    def greet(dev):
        pl.semaphore_signal(barrier, inc=1, device_id=dev, device_id_type=MESH)

    greet(partner)
    for d in range(1, R):
        greet((peer(d), c))
    pl.when(has_up)(lambda: greet(above))
    pl.when(has_dn)(lambda: greet(below))
    pl.semaphore_wait(barrier, R + jnp.where(has_up, 1, 0) + jnp.where(has_dn, 1, 0))

    def go_z(direction, j, p):
        ref = go_all.at[2 * j + k, pl.ds(p * piece, piece)]
        return remote(ref, ref, go_s.at[direction, j, p], go_r.at[j, p], (above, below)[direction])

    def go_pair(j, side):
        ref = go_all.at[2 * j + side]
        return remote(ref, ref, pg_s.at[j], pg_r.at[j], partner)

    def act_z(direction, j):
        ref = act_all.at[2 * j + k]
        return remote(ref, ref, ac_s.at[direction, j], ac_r.at[j], (above, below)[direction])

    def act_pair(j, side):
        ref = act_all.at[2 * j + side]
        return remote(ref, ref, pa_s.at[j], pa_r.at[j], partner)

    def row_all(ref, ssem, rsem, d, start, size):
        part = ref.at[ds(start, size), :]
        return remote(part, part, ssem, rsem, (peer(d), c))

    def rows_wait(ref, ssem, rsem, size):
        part = ref.at[pl.ds(0, size), :]
        return remote(part, part, ssem, rsem, (peer(1), c))

    def start_act(direction):
        act_z(direction, z).start()

    loads[0].wait()

    @pl.when(has_up)
    def _():
        for p in range(PIECES):
            go_z(0, z, p).start()

    @pl.when(has_dn)
    def _():
        for p in range(PIECES):
            go_z(1, z, p).start()

    go_pair(z, k).start()
    loads[1].wait()
    loads[2].wait()
    half = rows // 2

    def saved(ref, sems, along, owner, part, d):
        block = ref.at[ds(owner * rows + part * half, half), :]
        if along == 0:
            dev = row_a * lines + (row_b + d) % lines
        else:
            dev = (row_a + d) % side_len * lines + row_b
        return remote(block, block, sems[0], sems[1], (dev, c))

    arrays = (gate_all, up_all)
    for i, ref in enumerate(arrays):
        for d in range(1, lines):
            saved(ref, (gu_s.at[i, 0], gu_r.at[i, 0]), 0, r, 0, d).start()
        for d in range(1, side_len):
            saved(ref, (gu_s.at[i, 1], gu_r.at[i, 1]), 1, r, 1, d).start()
    for i, ref in enumerate(arrays):
        for d in range(1, side_len):
            saved(ref, (gu_s.at[i, 2], gu_r.at[i, 2]), 1, r, 0, d).start()
        for d in range(1, lines):
            saved(ref, (gu_s.at[i, 3], gu_r.at[i, 3]), 0, r, 1, d).start()

    def saved_wait(i, stage, count):
        part = arrays[i].at[pl.ds(0, count * half), :]
        return remote(part, part, gu_s.at[i, stage], gu_r.at[i, stage], partner)

    def forward_saved():
        for i, ref in enumerate(arrays):
            if lines > 1:
                saved_wait(i, 0, lines - 1).wait_recv()
            for e in range(1, lines):
                owner = row_a * lines + (row_b + e) % lines
                for d in range(1, side_len):
                    saved(ref, (gu_s.at[i, 4], gu_r.at[i, 4]), 1, owner, 0, d).start()
            if side_len > 1:
                saved_wait(i, 1, side_len - 1).wait_recv()
            for e in range(1, side_len):
                owner = (row_a + e) % side_len * lines + row_b
                for d in range(1, lines):
                    saved(ref, (gu_s.at[i, 5], gu_r.at[i, 5]), 0, owner, 1, d).start()

    counts = (
        lines - 1, side_len - 1, side_len - 1, lines - 1,
        (lines - 1) * (side_len - 1), (lines - 1) * (side_len - 1),
    )
    loads[4].wait()
    act_pair(z, k).start()
    pl.when(has_up & (z == 0))(lambda: start_act(0))
    pl.when(has_dn & (z == Z - 1))(lambda: start_act(1))

    def forward(s):
        for p in range(PIECES):
            @pl.when(z - s >= 0)
            def _():
                j = z - s
                go_z(0, j, p).wait_recv()
                pl.when(has_up)(lambda: go_z(0, j, p).start())
                if p == PIECES - 1:
                    go_pair(j, k).start()
                    pl.when(has_up & (s == z))(lambda: start_act(0))

            @pl.when(z + s < Z)
            def _():
                j = z + s
                go_z(1, j, p).wait_recv()
                pl.when(has_dn)(lambda: go_z(1, j, p).start())
                if p == PIECES - 1:
                    go_pair(j, k).start()
                    pl.when(has_dn & (s == Z - 1 - z))(lambda: start_act(1))

    def act_from(direction, j, relay):
        act_z(direction, j).wait_recv()
        if relay:
            act_z(direction, j).start()
        act_pair(j, k).start()

    to_edge = jnp.minimum(z, Z - 1 - z)
    lower = 2 * z < Z
    edge = to_edge == 0

    def act_relay(t):
        near = t - to_edge
        far = t - (Z - 1 - to_edge)
        near_ok = (near >= 1) & (near <= to_edge)
        far_ok = (far >= 1) & (far <= Z - 1 - to_edge) & jnp.logical_not(edge)
        pl.when(near_ok & lower)(lambda: act_from(0, z - near, True))
        pl.when(near_ok & jnp.logical_not(lower))(lambda: act_from(1, z + near, True))
        pl.when(far_ok & lower)(lambda: act_from(1, z + far, True))
        pl.when(far_ok & jnp.logical_not(lower))(lambda: act_from(0, z - far, True))

    def act_end(s):
        pl.when(edge & (z - s >= 0))(lambda: act_from(0, z - s, False))
        pl.when(edge & (z + s < Z))(lambda: act_from(1, z + s, False))

    ftile = tile_of(feats, 256)

    def partial_hidden(j):
        go_pair(j, 1 - k).wait_recv()
        lhs = go_all[pl.ds(2 * j, 2)].reshape(chunk, width)

        @pl.loop(0, feats // ftile)
        def _(f):
            cols = ds(f * ftile, ftile)
            res = lax.dot_general(lhs, wd[cols, :], CONTRACT_COLS, preferred_element_type=F32)
            part32[:, cols] = res
            part16[ds(j * chunk, chunk), cols] = res.astype(BF16)
            for d in range(1, R):
                src = part16.at[ds(j * chunk + peer(d) * own_rows, own_rows), cols]
                dst = rs_in.at[ds((j * (R - 1) + d - 1) * own_rows, own_rows), cols]
                remote(src, dst, rs_s.at[j], rs_r.at[j], (peer(d), c)).start()

        own32[ds(j * own_rows, own_rows), :] = part32[ds(r * own_rows, own_rows), :]

    def finish_sum(j):
        rows_wait(rs_in, rs_s.at[j], rs_r.at[j], (R - 1) * own_rows).wait_recv()
        mine = ds(j * chunk + r * own_rows, own_rows)
        total = own32[ds(j * own_rows, own_rows), :]
        for d in range(1, R):
            total = total + rs_in[ds((j * (R - 1) + d - 1) * own_rows, own_rows), :].astype(F32)
        gh_all[mine, :] = total.astype(BF16)
        for d in range(1, R):
            row_all(gh_all, ag_s.at[j], ag_r.at[j], d, j * chunk + r * own_rows, own_rows).start()

    eblock = 16

    def finish_gather(j):
        rows_wait(gh_all, ag_s.at[j], ag_r.at[j], (R - 1) * own_rows).wait_recv()

        @pl.loop(0, chunk // eblock)
        def _(b):
            at = pl.ds(pl.multiple_of(j * chunk + b * eblock, eblock), eblock)
            gate = gate_all[at, :].astype(F32)
            up = up_all[at, :].astype(F32)
            grad = gh_all[at, :].astype(F32)
            sigma = 1.0 / (1.0 + jnp.exp(-gate))
            hid_all[at, :] = (gate * sigma * up).astype(BF16)
            ggp_all[at, :] = (grad * up * sigma * (1.0 + gate * (1.0 - sigma))).astype(BF16)
            gup_all[at, :] = (grad * gate * sigma).astype(BF16)

    def gathered_saved():
        for i in range(2):
            for stage in range(2, 6):
                if counts[stage]:
                    saved_wait(i, stage, counts[stage]).wait_recv()

    def at_distance(s, step):
        pl.when(z - s >= 0)(lambda: step(z - s))
        if s > 0:
            pl.when(z + s < Z)(lambda: step(z + s))

    gtile = tile_of(wt, 256)

    half_line = Z // 2
    first = jnp.where(lower, 0, half_line)
    last = jnp.where(lower, half_line, 0)

    def input_tile(n, start, count):
        rows_at = ds(start * chunk, count * chunk, chunk)

        @pl.loop(0, wt // gtile)
        def _(t):
            at = ds(n * wt + t * gtile, gtile)
            res = lax.dot_general(ggp_all[rows_at, :], wg[at, :], CONTRACT_COLS, preferred_element_type=F32)
            res = res + lax.dot_general(gup_all[rows_at, :], wu[at, :], CONTRACT_COLS, preferred_element_type=F32)
            for j in range(count):
                for side in range(2):
                    low_row = (2 * j + side) * shard
                    gi[n, side, start + j, :, ds(t * gtile, gtile)] = res[low_row : low_row + shard]

    def pair_sum(n, late):
        at = pl.ds(last if late else first, half_line)
        return remote(gi.at[n, 1 - k, at], pair_in.at[n, at], pr_s.at[late, n], pr_r.at[late, n], partner)

    def early(n):
        input_tile(n, first, half_line)
        pair_sum(n, 0).start()

    def late(n):
        input_tile(n, last, half_line)
        pair_sum(n, 1).start()

    def z_copy(n, j, slot, dev):
        return remote(z_out.at[n, j], z_in.at[n, slot], z_s.at[n, j], z_r.at[n, slot], dev)

    def pass_on(n, j, fed, slot, dev):
        total = gi[n, k, j] + pair_in[n, j]
        if fed:
            z_copy(n, j, j, dev).wait_recv()
            total = total + z_in[n, j].astype(F32)
        z_out[n, j] = total.astype(BF16)
        z_copy(n, j, slot, dev).start()

    def move_up(n, j, fed):
        pass_on(n, j, fed, j, above)

    def move_down(n, j, fed):
        pass_on(n, j, fed, jnp.where(z - 1 == j, Z, j), below)

    def edge_serve(n, is_late):
        pair_sum(n, is_late).wait_recv()
        for j in range(Z - 1, half_line - 1, -1) if is_late else range(half_line - 1, 0, -1):
            pl.when(lower)(functools.partial(move_up, n, j, False))
        for j in range(half_line) if is_late else range(half_line, Z - 1):
            pl.when(jnp.logical_not(lower))(functools.partial(move_down, n, j, False))

    def mid_early(n):
        pair_sum(n, 0).wait_recv()
        for j in range(half_line - 1, 1, -1):
            pl.when((z < j) & lower)(functools.partial(move_up, n, j, True))
        for j in range(half_line, Z - 2):
            pl.when((z > j) & jnp.logical_not(lower))(functools.partial(move_down, n, j, True))

    def mid_late(n, near):
        if near:
            pair_sum(n, 1).wait_recv()
        for j in range(Z - 1, half_line - 1, -1):
            pl.when((z < j) & (lower == near))(functools.partial(move_up, n, j, True))
        for j in range(half_line):
            pl.when((z > j) & (lower != near))(functools.partial(move_down, n, j, True))

    def finish(n):
        total = gi[n, k, z] + pair_in[n, z]
        cols = pl.ds(n * wt, wt)
        gi[n, k, z] = total

        @pl.when(has_dn)
        def _():
            z_copy(n, z, z, below).wait_recv()
            gi[n, k, z] += z_in[n, z].astype(F32)

        @pl.when(has_up)
        def _():
            z_copy(n, z, Z, above).wait_recv()
            gi[n, k, z] += z_in[n, Z].astype(F32)

        gi_out[:, cols] = gi[n, k, z].astype(BF16)

    blocks = 4
    fb = feats // blocks
    wb = width // blocks
    nb = tile_of(width, 1024)

    def down_block(i):
        rows_at = pl.ds(i * fb, fb)

        @pl.loop(0, width // nb)
        def _(t):
            cols = ds(t * nb, nb)
            rhs = go_all[:, :, cols].reshape(tokens, nb)
            wd[rows_at, cols] = lax.dot_general(
                hid_all[:, rows_at], rhs, CONTRACT_ROWS, preferred_element_type=F32
            ).astype(BF16)

    def gate_block(i):
        gb = tile_of(wb, 256)

        @pl.loop(0, wb // gb)
        def _(t):
            cols = ds(i * wb + t * gb, gb)
            lhs = act_all[:, :, cols].reshape(tokens, gb)
            wg[cols, :] = lax.dot_general(
                lhs, ggp_all[...], CONTRACT_ROWS, preferred_element_type=F32
            ).astype(BF16)

    for s in range(Z):
        if s > 0:
            forward(s)
        if s == half_line + 1:
            pl.when(edge)(lambda: early(1))
        if s == 0:
            loads[3].wait()
        at_distance(s, partial_hidden)
        if s == 1:
            forward_saved()
        if s >= 2:
            act_relay(s)
        if s > 0:
            pl.when(jnp.logical_not(edge))(lambda: at_distance(s - 1, finish_sum))
        if s == min(2, Z - 1):
            gathered_saved()
            at_distance(0, finish_gather)
            if Z > 2:
                pl.when(edge)(lambda: at_distance(1, finish_gather))
            loads[5].wait()
            loads[6].wait()
        if s > 2:
            pl.when(jnp.logical_not(edge))(lambda: at_distance(s - 2, finish_gather))
            if s < Z - 1:
                pl.when(edge)(lambda: at_distance(s - 1, finish_gather))
        if s == half_line:
            pl.when(edge)(lambda: early(0))
        if s < Z - 1:
            pl.when(edge)(lambda: at_distance(s, finish_sum))
        if s == half_line:
            pl.when(edge)(lambda: edge_serve(0, 0))

    if Z > 2:
        pl.when(jnp.logical_not(edge))(lambda: at_distance(Z - 2, finish_gather))

    @pl.when(edge)
    def _():
        if half_line + 1 >= Z:
            early(1)
        edge_serve(1, 0)
        if Z > 3:
            at_distance(Z - 2, finish_gather)
        early(2)
        at_distance(Z - 1, finish_sum)
        edge_serve(2, 0)
        early(3)
        edge_serve(3, 0)
        at_distance(Z - 1, finish_gather)
        late(0)
        edge_serve(0, 1)
        for n in range(1, ntiles):
            late(n)
            edge_serve(n, 1)
        for s in range(1, Z - 1):
            act_end(s)
        for i in range(blocks):
            down_block(i)
        act_end(Z - 1)
        for j in range(Z):
            act_pair(j, 1 - k).wait_recv()
        for i in range(blocks):
            gate_block(i)

    @pl.when(jnp.logical_not(edge))
    def _():
        at_distance(Z - 1, finish_sum)
        early(0)
        act_relay(Z)
        at_distance(Z - 1, finish_gather)
        late(0)
        early(1)
        late(1)
        mid_early(0)
        mid_early(1)
        early(2)
        late(2)
        mid_early(2)
        down_block(0)
        down_block(1)
        mid_late(0, True)
        act_relay(Z + 1)
        early(3)
        late(3)
        mid_early(3)
        mid_late(1, True)
        mid_late(0, False)
        for t in range(Z + 2, 2 * Z - 2):
            act_relay(t)
        down_block(2)
        down_block(3)
        mid_late(2, True)
        mid_late(1, False)
        for j in range(Z):
            act_pair(j, 1 - k).wait_recv()
        gate_block(0)
        gate_block(1)
        mid_late(3, True)
        mid_late(2, False)
        gate_block(2)
        mid_late(3, False)
        gate_block(3)

    for n in range(ntiles):
        finish(n)

    for j in range(Z):
        go_pair(j, k).wait_send()
        act_pair(j, k).wait_send()
        rows_wait(part16, rs_s.at[j], rs_r.at[j], (R - 1) * own_rows).wait_send()
        rows_wait(gh_all, ag_s.at[j], ag_r.at[j], (R - 1) * own_rows).wait_send()

        @pl.when((z >= j) & has_up)
        def _():
            for p in range(PIECES):
                go_z(0, j, p).wait_send()
            act_z(0, j).wait_send()

        @pl.when((z <= j) & has_dn)
        def _():
            for p in range(PIECES):
                go_z(1, j, p).wait_send()
            act_z(1, j).wait_send()

        @pl.when(z != j)
        def _():
            for n in range(ntiles):
                z_copy(n, j, j, partner).wait_send()

    for i in range(2):
        for stage in range(6):
            if counts[stage]:
                saved_wait(i, stage, counts[stage]).wait_send()
    for n in range(ntiles):
        pair_sum(n, 0).wait_send()
        pair_sum(n, 1).wait_send()


def exchange(row_size, col_size, act, go, gate, up, wg, wu, wd):
    R, Z = row_size, col_size // 2
    shard, width = go.shape
    rows, feats = gate.shape
    tokens = shard * col_size
    own_rows = 2 * shard // R
    nt = COLUMN_TILES
    wt = width // nt
    hbm = pl.BlockSpec(memory_space=pltpu.HBM)
    vmem = pl.BlockSpec(memory_space=pltpu.VMEM)
    dma = pltpu.SemaphoreType.DMA
    sds = jax.ShapeDtypeStruct
    return pl.pallas_call(
        functools.partial(exchange_kernel, row_size, col_size),
        out_shape=[
            pltpu.VMEM((shard, width), BF16),
            pltpu.VMEM(wd.shape, BF16),
            pltpu.VMEM(wg.shape, BF16),
            pltpu.VMEM((col_size, shard, width), BF16),
            pltpu.VMEM((tokens, feats), BF16),
        ],
        in_specs=[hbm] * 7,
        out_specs=[vmem] * 5,
        scratch_shapes=[
            pltpu.VMEM((col_size, shard, width), BF16),
            pltpu.VMEM((tokens, feats), BF16),
            pltpu.VMEM((tokens, feats), BF16),
            pltpu.VMEM(wu.shape, BF16),
            pltpu.VMEM((tokens, feats), BF16),
            pltpu.VMEM((tokens, feats), BF16),
            pltpu.VMEM((2 * shard, feats), F32),
            pltpu.VMEM((Z * own_rows, feats), F32),
            pltpu.VMEM((tokens, feats), BF16),
            pltpu.VMEM((Z * (R - 1) * own_rows, feats), BF16),
            pltpu.VMEM((tokens, feats), BF16),
            pltpu.VMEM((nt, 2, Z, shard, wt), F32),
            pltpu.VMEM((nt, Z, shard, wt), F32),
            pltpu.VMEM((nt, Z + 1, shard, wt), BF16),
            pltpu.VMEM((nt, Z, shard, wt), BF16),
            dma((7,)),
            dma((Z, PIECES)), dma((2, Z, PIECES)), dma((Z,)), dma((Z,)),
            dma((Z,)), dma((2, Z)), dma((Z,)), dma((Z,)),
            dma((2, 6)), dma((2, 6)),
            dma((Z,)), dma((Z,)), dma((Z,)), dma((Z,)),
            dma((2, nt)), dma((2, nt)), dma((nt, Z + 1)), dma((nt, Z)),
        ],
        compiler_params=pltpu.CompilerParams(
            collective_id=0, has_side_effects=True, vmem_limit_bytes=39 << 20
        ),
        name="exchange",
    )(*(pltpu.with_memory_space_constraint(x, pltpu.HBM) for x in (act, go, gate, up, wg, wu, wd)))


def last_kernel(steps, lhs, rhs, down, gate, inp, out, down_out, gate_out, inp_out, sems):
    i = pl.program_id(0)

    def copies(step):
        for a, (src, dst) in enumerate(((down, down_out), (gate, gate_out), (inp, inp_out))):
            part = src.shape[0] // steps
            at = pl.ds(pl.multiple_of(step * part, part), part)
            yield pltpu.make_async_copy(src.at[at], dst.at[at], sems.at[a, step])

    for copy in copies(i):
        copy.start()

    cols = pl.ds(pl.multiple_of(i * out.shape[0], out.shape[0]), out.shape[0])
    out[...] = lax.dot_general(
        lhs[:, :, cols].reshape(rhs.shape[0], out.shape[0]), rhs[...], CONTRACT_ROWS, preferred_element_type=F32
    ).astype(BF16)

    @pl.when(i == steps - 1)
    def _():
        for step in range(steps):
            for copy in copies(step):
                copy.wait()


def last_grad(act, gup, down, gate, inp):
    cols, shard, width = act.shape
    tokens, feats = gup.shape
    tile = tile_of(width, 512)
    steps = width // tile
    sds = jax.ShapeDtypeStruct
    vmem = pl.BlockSpec(memory_space=pltpu.VMEM)
    hbm = pl.BlockSpec(memory_space=pltpu.HBM)
    return pl.pallas_call(
        functools.partial(last_kernel, steps),
        grid=(steps,),
        out_shape=[sds(x, BF16) for x in ((width, feats), down.shape, gate.shape, inp.shape)],
        in_specs=[
            vmem,
            vmem,
            vmem,
            vmem,
            vmem,
        ],
        out_specs=[pl.BlockSpec((tile, feats), lambda i: (i, 0)), hbm, hbm, hbm],
        scratch_shapes=[pltpu.SemaphoreType.DMA((3, steps))],
        compiler_params=pltpu.CompilerParams(vmem_limit_bytes=16 << 20),
        name="last_grad",
    )(*(pltpu.with_memory_space_constraint(x, pltpu.VMEM) for x in (act, gup, down, gate, inp)))


def local(row_size, col_size, activations, grad_output, gate_pre, up_pre, w_gate, w_up, w_down):
    grad_input, grad_down, grad_gate, act_all, gup = exchange(
        row_size, col_size, activations, grad_output, gate_pre, up_pre, w_gate, w_up, w_down
    )
    grad_up, grad_down, grad_gate, grad_input = last_grad(act_all, gup, grad_down, grad_gate, grad_input)
    return grad_input, grad_gate, grad_up, grad_down


def solution(mesh):
    in_specs = (
        P("col", "row"), P("col", "row"), P("row", "col"), P("row", "col"),
        P("row", "col"), P("row", "col"), P("col", "row"),
    )
    out_specs = (P("col", "row"), P("row", "col"), P("row", "col"), P("col", "row"))
    body = functools.partial(local, mesh.shape["row"], mesh.shape["col"])
    return jax.shard_map(body, mesh=mesh, in_specs=in_specs, out_specs=out_specs, check_vma=False)
```
